32 devices in a mesh: expert: 32 (over z, y, x, core).
Axes of the slice: x: 2, y: 2, z: 4, core: 2. Of those that a mesh axis runs over, the one named last changes fastest.
Arguments:
- tokens: bfloat16 [4096, 3584], P('expert'), may hold values from -6 to 6
- cotangent: bfloat16 [4096, 3584], P('expert'), may hold values from -6 to 6
- routes: int32 [4096, 8], P('expert'), may hold values from 0 to 15, all different within a row; in each aligned block of 128 rows (0 to 127, 128 to 255, ...) at most 80 rows name the same one
- gates: bfloat16 [4096, 8], P('expert'), may hold values from 0.049804688 to 0.29882812
- previous_row: int32 [16], replicated, may hold values from 0 to 15, each once
- gu_payload: bfloat16 [16, 3584, 2048], P(None, 'expert'), may hold values from -0.09375 to 0.09375
- gu_scales: float32 [16, 28, 16], replicated, may hold values from 0.5 to 2
- down_payload: bfloat16 [16, 1024, 3584], P(None, 'expert'), may hold values from -0.1875 to 0.1875
- down_scales: float32 [16, 8, 28], replicated, may hold values from 0.5 to 2
Outputs:
- layer_out: bfloat16 [4096, 3584], P('expert')
- gate_grad: float32 [4096, 8], P('expert')
The draws below stay inside these ranges and needn't reach their ends.
Inputs may be any that keep to these rules, and one draw needn't show every extreme that they name: `routes`: each token names 8 different experts; among the tokens of one device no expert is named by more than 80 of them, and in some devices' tokens one expert is named by exactly 80. `previous_row`: each stored row holds exactly one expert.
All inputs are finite; a program needn't handle non-finite values.
Results may differ from the reference program's by a relative error of at most 0.0076.
Values may be sent and summed in bfloat16 or wider, within the bound.
A program may use at most 256 MiB of HBM per device.

```python
import math
import jax
import jax.numpy as jnp
import numpy as np
from jax import lax

D = 3584
FF = 1024
TOP = 8
TOK_DEV = 128
SLOTS = 32
EXPERTS = 16
MOST = 80
TOKENS = 4096


def steps_of(key, shape, cuts, smallest, largest):
    level, own = 1.0, jax.random.fold_in(key, 6)
    for axis_at, blocks in cuts:
        heights = jnp.exp(jax.random.uniform(jax.random.fold_in(own, axis_at), (blocks,), jnp.float32, smallest / len(cuts), largest / len(cuts)))
        level = level * jnp.repeat(heights, shape[axis_at] // blocks).reshape([-1 if axis == axis_at else 1 for axis in range(len(shape))])
    return level


def deal_out(own_key, own, number, rows, amount, top, limit, skew):
    sequence = jax.random.permutation(own_key, amount)
    heavy_load, ordinary = shares(amount, rows * top, limit, skew, True), shares(amount, rows * top, limit, skew, False)
    places = jnp.arange(amount)

    def named(lengths, rotation):
        used = int((lengths > 0).sum())
        fixed = max(1, used // 4)
        shifted = fixed + (places - fixed + rotation * (used - fixed)) % max(1, amount - fixed)
        return jnp.zeros((amount,), jnp.int32).at[sequence[jnp.where(places < fixed, places, shifted)]].set(jnp.asarray(lengths, jnp.int32))

    lengths = jnp.where(number % 4 == 0, named(heavy_load, number // 4), named(ordinary, number - number // 4 - 1))
    mixed = jax.random.permutation(jax.random.fold_in(own, 3), amount)
    source_of, sink = mixed[0:amount // 2 * 2:2], mixed[1:amount // 2 * 2:2]
    room = jnp.minimum(lengths[source_of] - 1, limit - lengths[sink]) // 2
    room = jnp.where((source_of == sequence[0]) | (sink == sequence[0]) | (lengths[sink] == 0), 0, jnp.maximum(room, 0))
    shifted = jax.random.randint(jax.random.fold_in(own, 4), (amount // 2,), 0, 1 << 20) % (room + 1)
    lengths = lengths.at[source_of].add(-shifted).at[sink].add(shifted)
    labels = jnp.searchsorted(jnp.cumsum(lengths), jnp.arange(rows * top), side="right").astype(jnp.int32)
    grid = labels.reshape(top, rows).T
    grid = grid[jax.random.permutation(jax.random.fold_in(own, 1), rows)]
    rotation = jax.random.randint(jax.random.fold_in(own, 2), (rows, 1), 0, top)
    return jnp.take_along_axis(grid, (jnp.arange(top)[None, :] + rotation) % top, axis=1)


def shares(amount, total, most, skew, full):
    weights = [(1 << 20) // math.isqrt(standing ** skew) + 1 for standing in range(1, amount + 1)]
    largest = most if full else min(most, max(-(-total // amount), total * weights[0] // sum(weights)))
    least = 1 if total - largest >= amount - 1 else 0
    holding, spare = [largest] + [least] * (amount - 1), total - largest - least * (amount - 1)
    while spare > 0:
        free = [i for i in range(1, amount) if holding[i] < largest] or [i for i in range(1, amount) if holding[i] < most]
        whole, left = sum([weights[i] for i in free]), spare
        for i in free:
            more = min(most - holding[i], max(1, left * weights[i] // whole), spare)
            holding[i] = holding[i] + more
            spare = spare - more
    return np.array(holding)


def normal_values(own_key, shape, spread, bound, cuts=(), held_as=jnp.bfloat16):
    values = spread * jax.random.normal(own_key, shape, jnp.float32)
    if cuts:
        values = values * steps_of(own_key, shape, cuts, -0.22, 0.18)
    return jnp.clip(values, -bound, bound).astype(held_as)


def setup_inputs(seed: int = 0) -> dict:
    seeds = jax.random.split(jax.random.key(seed), 10)
    tokens = normal_values(seeds[0], (TOKENS, D), 1.0, 6.0, ((0, 32),))
    cotangent = normal_values(seeds[1], (TOKENS, D), 1.0, 6.0, ((0, 32),))
    routes_keys = jax.random.split(jax.random.fold_in(seeds[2], 1), TOKENS // TOK_DEV)
    routes_turns = jax.random.permutation(jax.random.fold_in(seeds[2], 3), TOKENS // TOK_DEV)
    routes = jax.vmap(lambda own, number: deal_out(jax.random.fold_in(seeds[2], 2), own, number, TOK_DEV, EXPERTS, TOP, MOST, 2))(routes_keys, routes_turns).reshape((TOKENS, TOP))
    gates = jnp.clip(0.049804688 + 0.24902344 * jax.random.uniform(seeds[3], (TOKENS, TOP), jnp.float32) ** steps_of(seeds[3], (TOKENS, TOP), ((0, 32),), -0.2, 0.2), 0.049804688, 0.29882812).astype(jnp.bfloat16)
    previous_row = jax.random.permutation(seeds[4], EXPERTS).astype(jnp.int32)
    gu_payload = normal_values(seeds[5], (EXPERTS, D, 2 * FF), D ** -0.5, 0.09375, ((1, 32),))
    gu_scales = jnp.clip(jnp.exp(jax.random.uniform(seeds[6], (EXPERTS, D // 128, 2 * FF // 128), jnp.float32, math.log(0.5), math.log(2.0))), 0.5, 2.0)
    down_payload = normal_values(seeds[7], (EXPERTS, FF, D), FF ** -0.5, 0.1875, ((1, 32),))
    down_scales = jnp.clip(jnp.exp(jax.random.uniform(seeds[8], (EXPERTS, FF // 128, D // 128), jnp.float32, math.log(0.5), math.log(2.0))), 0.5, 2.0)
    return {"tokens": tokens, "cotangent": cotangent, "routes": routes, "gates": gates, "previous_row": previous_row, "gu_payload": gu_payload, "gu_scales": gu_scales, "down_payload": down_payload, "down_scales": down_scales}


def dequantize(payload, scales):
    expanded = jnp.repeat(jnp.repeat(scales, 128, axis=0), 128, axis=1)
    return (payload.astype(jnp.float32) * expanded).astype(jnp.bfloat16)


def reference(tokens, cotangent, routes, gates, previous_row, gu_payload, gu_scales, down_payload, down_scales):
    flat_routes = routes.reshape(-1)
    route_count = flat_routes.shape[0]
    row_limit = MOST * SLOTS
    token_of = jnp.arange(route_count, dtype=jnp.int32) // TOP
    route_ids = jnp.arange(route_count, dtype=jnp.int32)

    def one_expert(gathered, expert):
        is_match = (flat_routes == expert).astype(jnp.int32)
        route_rank = jnp.cumsum(is_match) - 1
        target = jnp.where(is_match == 1, route_rank, row_limit).astype(jnp.int32)
        token_table = jnp.zeros((row_limit,), jnp.int32).at[target].set(token_of, mode="drop")
        route_table = jnp.full((row_limit,), route_count, jnp.int32).at[target].set(route_ids, mode="drop")
        stored = previous_row[expert]
        w_gu = dequantize(gu_payload[stored], gu_scales[stored])
        w_down = dequantize(down_payload[stored], down_scales[stored])
        hidden = jnp.dot(tokens[token_table], w_gu, preferred_element_type=jnp.float32)
        active = (jax.nn.silu(hidden[:, :FF]) * hidden[:, FF:]).astype(jnp.bfloat16)
        result = jnp.dot(active, w_down, preferred_element_type=jnp.float32).astype(jnp.bfloat16)
        return gathered.at[route_table].set(result, mode="drop"), None

    start = jnp.zeros((route_count, D), jnp.bfloat16)
    per_route, unused = lax.scan(one_expert, start, jnp.arange(EXPERTS, dtype=jnp.int32))
    stacked = per_route.reshape(-1, TOP, D).astype(jnp.float32)
    layer_out = jnp.einsum("tk,tkd->td", gates.astype(jnp.float32), stacked).astype(jnp.bfloat16)
    gate_grad = jnp.einsum("td,tkd->tk", cotangent.astype(jnp.float32), stacked)
    return layer_out, gate_grad
```

```python
import jax
import jax.numpy as jnp
from jax import lax
from jax.sharding import PartitionSpec as P


def dequantize(payload, scales):
    expanded = jnp.repeat(jnp.repeat(scales, 128, axis=0), 128, axis=1)
    return (payload.astype(jnp.float32) * expanded).astype(jnp.bfloat16)


def plan(routes, gates, previous_row, most):
    local_count = routes.shape[0]
    rows = previous_row.shape[0]
    ids = jnp.arange(rows, dtype=jnp.int32)
    row_of = jnp.sum(jnp.where(routes[:, :, None] == ids, previous_row, 0), axis=2)
    hits = row_of[:, :, None] == ids
    chosen = jnp.sum(hits.astype(jnp.float32), axis=1)
    gate_of = jnp.sum(jnp.where(hits, gates.astype(jnp.float32)[:, :, None], 0.0), axis=1)
    places = jnp.arange(local_count, dtype=jnp.int32)
    before = (places[:, None] < places[None, :]).astype(jnp.bfloat16)
    rank = jnp.einsum(
        "ut,us->st", before, chosen.astype(jnp.bfloat16), preferred_element_type=jnp.float32
    ).astype(jnp.int32)
    slots = jnp.arange(most, dtype=jnp.int32)
    picked = (rank[:, None, :] == slots[None, :, None]) & (chosen.T[:, None, :] > 0)
    select = picked.astype(jnp.bfloat16)
    weigh = jnp.where(picked, gate_of.T[:, None, :], 0.0).astype(jnp.bfloat16)
    return hits, select.reshape(rows * most, local_count), weigh.reshape(rows * most, local_count)


def shards(
    tokens, cotangent, routes, gates, previous_row, gu_payload, gu_scales, down_payload, down_scales
):
    local_count, model_width = tokens.shape
    top = routes.shape[1]
    hidden_width = gu_payload.shape[2] // 2
    devices = lax.axis_size("expert")
    device_id = lax.axis_index("expert")
    experts = previous_row.shape[0]
    copies = devices // experts
    groups = [[c * experts + i for i in range(experts)] for c in range(copies)]
    most = local_count * top * 5 // (4 * experts)
    hits, select, weigh = plan(routes, gates, previous_row, most)
    outgoing = jnp.dot(select, tokens, preferred_element_type=jnp.float32).astype(jnp.bfloat16)
    outgoing = outgoing.reshape(experts, most, model_width)
    arrived = lax.all_to_all(
        outgoing, "expert", split_axis=0, concat_axis=0, tiled=True, axis_index_groups=groups
    )
    send_gate = jnp.concatenate([gu_payload] * copies, axis=0)
    send_down = jnp.concatenate([down_payload] * copies, axis=0)
    got_gate = lax.all_to_all(send_gate, "expert", split_axis=0, concat_axis=0, tiled=True)
    got_down = lax.all_to_all(send_down, "expert", split_axis=0, concat_axis=0, tiled=True)
    own_row = device_id % experts
    w_gu = dequantize(got_gate.reshape(model_width, 2 * hidden_width), gu_scales[own_row])
    w_down = dequantize(got_down.reshape(hidden_width, model_width), down_scales[own_row])
    row_block = arrived.reshape(-1, model_width)
    hidden = jnp.dot(row_block, w_gu, preferred_element_type=jnp.float32)
    active = (jax.nn.silu(hidden[:, :hidden_width]) * hidden[:, hidden_width:]).astype(jnp.bfloat16)
    result = jnp.dot(active, w_down, preferred_element_type=jnp.float32).astype(jnp.bfloat16)
    returned = lax.all_to_all(
        result.reshape(arrived.shape),
        "expert",
        split_axis=0,
        concat_axis=0,
        tiled=True,
        axis_index_groups=groups,
    ).reshape(-1, model_width)
    layer_out = jnp.einsum(
        "st,sd->td", weigh, returned, preferred_element_type=jnp.float32
    ).astype(jnp.bfloat16)
    dots = jnp.einsum("sd,td->st", returned, cotangent, preferred_element_type=jnp.float32)
    dots = jnp.sum(
        jnp.where(select > 0, dots, 0.0).reshape(experts, most, local_count), axis=1
    )
    gate_grad = jnp.sum(jnp.where(hits, dots.T[:, None, :], 0.0), axis=2)
    return (layer_out, gate_grad)


def solution(mesh):
    in_specs = (
        P("expert", None),
        P("expert", None),
        P("expert", None),
        P("expert", None),
        P(),
        P(None, "expert", None),
        P(),
        P(None, "expert", None),
        P(),
    )
    out_specs = (P("expert", None), P("expert", None))
    return jax.shard_map(shards, mesh=mesh, in_specs=in_specs, out_specs=out_specs, check_vma=False)
```
